256 devices in a mesh: tm: 8 (over z), seq: 32 (over y, x, core).
Axes of the slice: x: 4, y: 4, z: 8, core: 2. Of those that a mesh axis runs over, the one named last changes fastest.
Arguments:
- states: float32 [64, 1536, 64], P('tm', 'seq'), may hold values from -11 to 11
- first_state: float32 [1536, 64], P('seq'), may hold values from -6 to 6
- now_step: int32 [64], P('tm'), may hold values from 1 to 960, as said below
- next_step: int32 [64], P('tm'), may hold values from 0 to 959, as said below
- embed_weight: bfloat16 [64, 1536], replicated, may hold values from -0.75 to 0.75
- mod_weight: bfloat16 [256, 4608], replicated, may hold values from -0.375 to 0.375
- qkv_weight: bfloat16 [1536, 12, 384], P('seq'), may hold values from -1 to 1
- out_weight: bfloat16 [1536, 1536], P('seq'), may hold values from -0.15625 to 0.15625
- final_weight: bfloat16 [1536, 64], replicated, may hold values from -0.15625 to 0.15625
Outputs:
- advanced: float32 [64, 1536, 64], P('tm', 'seq')
- errors: float32 [64], P('tm')
The draws below stay inside these ranges and needn't reach their ends.
Inputs may be any that keep to these rules, and one draw needn't show every extreme that they name: now_step[0] = 960 and now_step[j + 1] = next_step[j]. next_step[j] is now_step[j] minus a gap of 1 to 15.
All inputs are finite; a program needn't handle non-finite values.
Results may differ from the reference program's by a relative error of at most 0.002.
Values may be sent and summed in bfloat16 or wider, within the bound.
A program may use at most 64 MiB of HBM per device.

```python
import math
import jax
import jax.numpy as jnp
from jax import lax

D = 1536
HEADS = 12
FREQ = 256
HD = 128
CH = 64
L = 1536
WIN = 64


def plan_gaps(key):
    largest_gap = 960 // WIN
    return jax.random.randint(jax.random.fold_in(key, 7), (WIN,), 1, largest_gap + 1)


def draw_now_step(key, part):
    step_gaps = plan_gaps(key)
    return (960 - jnp.cumsum(step_gaps) + step_gaps).astype(jnp.int32)


def draw_next_step(key, part):
    step_gaps = plan_gaps(key)
    return (960 - jnp.cumsum(step_gaps)).astype(jnp.int32)


def draw_states(key, part):
    value_key = jax.random.fold_in(key, 21)
    jitter_key = jax.random.fold_in(key, 22)
    position = jnp.arange(L, dtype=jnp.float32) / max(L - 1, 1)
    jitter = jnp.exp(jax.random.uniform(jitter_key, (WIN, L, 1), jnp.float32, math.log(0.7), math.log(1.4)))
    token_ramp = 0.6 + 1.2 * position
    entries = jnp.clip(jax.random.normal(value_key, (WIN, L, CH), jnp.float32), -4.0, 4.0)
    return entries * token_ramp[None, :, None] * jitter


def draw_qkv_weight(key, part):
    entries = jnp.clip(jax.random.normal(jax.random.fold_in(key, 31), (D, HEADS, 3 * HD), jnp.float32), -4.0, 4.0) * D ** (-0.5)
    return jnp.clip(entries, -1.0, 1.0).astype(jnp.bfloat16)


def levels(own_key, extent, pieces, low, largest):
    gain = 1.0
    for dim, blocks in pieces:
        steps = jax.random.uniform(jax.random.fold_in(jax.random.fold_in(own_key, 6), dim), (blocks,), jnp.float32, low / len(pieces), largest / len(pieces))
        gain = gain * jnp.repeat(jnp.exp(steps), extent[dim] // blocks).reshape((-1,) + (1,) * (len(extent) - 1 - dim))
    return gain


def bell_draw(rng, dims, deviation, bound, shards=(), held_as=jnp.bfloat16):
    array = deviation * jax.random.normal(rng, dims, jnp.float32)
    if shards:
        array = array * levels(rng, dims, shards, -0.22, 0.18)
    return jnp.clip(array, -bound, bound).astype(held_as)


def setup_inputs(seed: int = 0) -> dict:
    key_of = jax.random.split(jax.random.key(seed), 10)
    states = draw_states(jax.random.fold_in(key_of[9], 71), 0)
    first_state = bell_draw(key_of[1], (L, CH), 1.0, 6.0, ((0, 32),), jnp.float32)
    now_step = draw_now_step(jax.random.fold_in(key_of[9], 71), 0)
    next_step = draw_next_step(jax.random.fold_in(key_of[9], 71), 0)
    embed_weight = bell_draw(key_of[4], (CH, D), CH ** -0.5, 0.75)
    mod_weight = bell_draw(key_of[5], (FREQ, 3 * D), FREQ ** -0.5, 0.375)
    qkv_weight = draw_qkv_weight(jax.random.fold_in(key_of[9], 71), 0)
    out_weight = bell_draw(key_of[7], (D, D), D ** -0.5, 0.15625, ((0, 32),))
    final_weight = bell_draw(key_of[8], (D, CH), D ** -0.5, 0.15625)
    return {"states": states, "first_state": first_state, "now_step": now_step, "next_step": next_step, "embed_weight": embed_weight, "mod_weight": mod_weight, "qkv_weight": qkv_weight, "out_weight": out_weight, "final_weight": final_weight}


def layer_norm(rows):
    row_mean = lax.optimization_barrier(jnp.mean(rows, axis=-1, keepdims=True))
    centered = rows - row_mean
    variance = lax.optimization_barrier(jnp.mean(centered * centered, axis=-1, keepdims=True))
    return centered * lax.rsqrt(variance + 1e-06)

def alpha_bar(step_ids):
    fraction = (step_ids.astype(jnp.float32) / 1000.0 + 0.008) / 1.008
    return jnp.cos(fraction * (math.pi / 2)) ** 2

def coefficients(now_step, next_step):
    alpha_now = alpha_bar(now_step)
    alpha_next = alpha_bar(next_step)
    step_ratio = jnp.sqrt(alpha_next / alpha_now)
    keep_coef = step_ratio - 1.0
    noise_coef = jnp.sqrt(1.0 - alpha_next) - step_ratio * jnp.sqrt(1.0 - alpha_now)
    return (keep_coef, noise_coef)

def modulation(step_ids, mod_weight):
    half_freq = mod_weight.shape[0] // 2
    frequency = jnp.exp(-math.log(10000.0) * jnp.arange(half_freq, dtype=jnp.float32) / half_freq)
    angles = step_ids.astype(jnp.float32)[:, None] * frequency[None, :]
    time_embed = jnp.concatenate([jnp.cos(angles), jnp.sin(angles)], axis=1).astype(jnp.bfloat16)
    return jnp.dot(time_embed, mod_weight, preferred_element_type=jnp.float32)

def attend_one(pair_item):
    hdim = pair_item.shape[1] // 3
    length = pair_item.shape[0]
    query_rows = 512 if length % 512 == 0 else length
    queries = pair_item[:, :hdim]
    key_rows = pair_item[:, hdim:2 * hdim]
    values = pair_item[:, 2 * hdim:]

    def one_block(query_block):
        scores = jnp.dot(query_block, key_rows.T, preferred_element_type=jnp.float32) * hdim ** (-0.5)
        row_max = lax.optimization_barrier(jnp.max(scores, axis=1, keepdims=True))
        exponent = jnp.exp(scores - row_max)
        weights = (exponent / lax.optimization_barrier(jnp.sum(exponent, axis=1, keepdims=True))).astype(jnp.bfloat16)
        return jnp.dot(weights, values, preferred_element_type=jnp.float32).astype(jnp.bfloat16)
    blocks_out = lax.map(one_block, queries.reshape(length // query_rows, query_rows, hdim))
    return blocks_out.reshape(length, hdim)

def reference(states, first_state, now_step, next_step, embed_weight, mod_weight, qkv_weight, out_weight, final_weight):
    previous = jnp.concatenate([first_state[None], states[:-1]], axis=0)
    keep_coef, noise_coef = coefficients(now_step, next_step)
    modulated_all = modulation(now_step, mod_weight)

    def one_step(inputs):
        prev_state, mod_row = inputs
        shift_mod = mod_row[:D]
        scale_mod = mod_row[D:2 * D]
        gate_mod = mod_row[2 * D:]
        residual = jnp.dot(prev_state.astype(jnp.bfloat16), embed_weight, preferred_element_type=jnp.float32)
        modulated = (layer_norm(residual) * (1.0 + scale_mod[None, :]) + shift_mod[None, :]).astype(jnp.bfloat16)
        projected = jnp.dot(modulated, qkv_weight.reshape(D, HEADS * 3 * HD), preferred_element_type=jnp.float32)
        projected = projected.astype(jnp.bfloat16).reshape(L, HEADS, 3 * HD)
        heads_out = lax.map(attend_one, jnp.transpose(projected, (1, 0, 2)))
        flattened = jnp.transpose(heads_out, (1, 0, 2)).reshape(L, D)
        projection = jnp.dot(flattened, out_weight, preferred_element_type=jnp.float32)
        updated = residual + gate_mod[None, :] * projection
        normed_out = layer_norm(updated).astype(jnp.bfloat16)
        return jnp.dot(normed_out, final_weight, preferred_element_type=jnp.float32)
    noise_pred = lax.map(one_step, (previous, modulated_all))
    drift_terms = keep_coef[:, None, None] * previous + noise_coef[:, None, None] * noise_pred
    advanced = first_state[None] + jnp.cumsum(drift_terms, axis=0)
    difference = advanced - states
    errors = lax.optimization_barrier(jnp.mean(difference * difference, axis=(1, 2)))
    return (advanced, errors)
```

```python
import math

import jax
import jax.numpy as jnp
from jax import lax
from jax.experimental import pallas as pl
from jax.experimental.pallas import tpu as pltpu
from jax.sharding import PartitionSpec as P

MESH = pl.DeviceIdType.MESH
F32 = jnp.float32
BF16 = jnp.bfloat16

PLANES = 8
ROWS = 4
COLS = 4
PEERS = 32
STEPS = 8
TOK = 48
PACK = 16
CH = 64
D = 1536
HD = 128
HEADS = 12
GROUP = 3
QTOK = 384
QROW = 128
LANES = 256


def alpha_bar(step_ids):
    fraction = (step_ids.astype(F32) / 1000.0 + 0.008) / 1.008
    return jnp.cos(fraction * (math.pi / 2)) ** 2


def coefficients(now_step, next_step):
    alpha_now = alpha_bar(now_step)
    alpha_next = alpha_bar(next_step)
    step_ratio = jnp.sqrt(alpha_next / alpha_now)
    keep_coef = step_ratio - 1.0
    noise_coef = jnp.sqrt(1.0 - alpha_next) - step_ratio * jnp.sqrt(1.0 - alpha_now)
    return (keep_coef, noise_coef)


def modulation(step_ids, mod_weight):
    half_freq = mod_weight.shape[0] // 2
    frequency = jnp.exp(-math.log(10000.0) * jnp.arange(half_freq, dtype=F32) / half_freq)
    angles = step_ids.astype(F32)[:, None] * frequency[None, :]
    time_embed = jnp.concatenate([jnp.cos(angles), jnp.sin(angles)], axis=1).astype(BF16)
    return jnp.dot(time_embed, mod_weight, preferred_element_type=F32)


def await_bytes(ref, sem):
    pltpu.make_async_copy(ref, ref, sem).wait()


def layer_norm(rows):
    row_mean = jnp.mean(rows, axis=-1, keepdims=True)
    centered = rows - row_mean
    variance = jnp.mean(centered * centered, axis=-1, keepdims=True)
    return centered * lax.rsqrt(variance + 1e-06)


def pack(tokens):
    first = jnp.concatenate([tokens[0:PACK], tokens[PACK : 2 * PACK]], axis=1)
    second = jnp.concatenate([tokens[2 * PACK :], jnp.zeros((PACK, CH), F32)], axis=1)
    return jnp.concatenate([first, second], axis=1)


class Spread:
    def __init__(self, place, pieces, whole, recv, send, send_y, natural):
        self.z, self.x, self.y, self.c, self.parity = place
        self.pieces, self.whole, self.natural = pieces, whole, natural
        self.recv, self.send, self.send_y = recv, send, send_y

    def up(self, k):
        return self.parity + 2 * k if k < 2 else (1 - self.parity) + 2 * (k - 2)

    def slot(self, k, xx, cc):
        major = lax.rem(self.y + self.up(k), ROWS) if self.natural else k
        return major * 8 + xx * 2 + cc

    def rows(self, slot):
        return self.whole.at[pl.ds(pl.multiple_of(slot * TOK, 16), TOK)]

    def await_slot(self, slot):
        await_bytes(self.rows(slot), self.recv.at[slot])

    def stage_y(self):
        for k in range(2):
            up = self.up(k)
            target = lax.rem(self.y - up + ROWS, ROWS)
            here = self.slot(k, self.x, self.c)
            there = (self.y if self.natural else k) * 8 + self.x * 2 + self.c
            source = self.pieces.at[target] if self.pieces.shape[0] > 1 else self.pieces.at[0]

            def remote():
                pltpu.make_async_remote_copy(
                    source, self.rows(there), self.send_y, self.recv.at[there],
                    device_id=(self.z, target * 8 + self.x * 2 + self.c), device_id_type=MESH,
                ).start()

            if k == 0:
                pl.when(self.parity == 1)(remote)

                @pl.when(self.parity == 0)
                def _():
                    pltpu.make_async_copy(source, self.rows(here), self.recv.at[here]).start()
            else:
                remote()

    def pass_on(self, slot, there, plane, xx, cc):
        pltpu.make_async_remote_copy(
            self.rows(slot), self.rows(there), self.send, self.recv.at[there],
            device_id=(plane, self.y * 8 + xx * 2 + cc), device_id_type=MESH,
        ).start()

    def side(self, by):
        return lax.rem(self.x + by + COLS, COLS)

    def to_plane(self, k, xx):
        plane = lax.rem(self.z + (1 if k == 0 else PLANES - 1), PLANES)
        slot = self.slot(k, xx, self.c)
        there = slot if self.natural else slot + 16
        self.pass_on(slot, there, plane, self.x, self.c)

    def to_sibling(self, slot):
        self.pass_on(slot, slot, self.z, self.x, 1 - self.c)

    def own(self, k):
        slot = self.slot(k, self.x, self.c)
        self.await_slot(slot)
        self.pass_on(slot, slot, self.z, self.side(1), self.c)
        self.pass_on(slot, slot, self.z, self.side(-1), self.c)
        self.to_plane(k, self.x)
        self.to_sibling(slot)

    def from_left(self, k):
        slot = self.slot(k, self.side(-1), self.c)
        self.await_slot(slot)
        if k == 0:
            self.pass_on(slot, slot, self.z, self.side(1), self.c)
        self.to_plane(k, self.side(-1))
        self.to_sibling(slot)

    def from_right(self, k):
        slot = self.slot(k, self.side(1), self.c)
        self.await_slot(slot)
        if k == 1:
            self.pass_on(slot, slot, self.z, self.side(-1), self.c)
        self.to_plane(k, self.side(1))
        self.to_sibling(slot)

    def far(self, k):
        slot = self.slot(k, self.side(2), self.c)
        self.await_slot(slot)
        self.to_plane(k, self.side(2))
        self.to_sibling(slot)

    def from_plane(self, k, by):
        slot = self.slot(k, self.side(by), self.c)
        self.await_slot(slot)
        self.to_sibling(slot)

    def await_sibling(self, k):
        for xx in range(COLS):
            self.await_slot(self.slot(k, xx, 1 - self.c))

    def finish(self):
        await_bytes(self.whole.at[pl.ds(0, 30 * TOK)], self.send)
        one = self.whole.at[pl.ds(0, TOK)]
        two = self.whole.at[pl.ds(0, 2 * TOK)]

        @pl.when(self.parity == 0)
        def _():
            await_bytes(one, self.send_y)

        @pl.when(self.parity == 1)
        def _():
            await_bytes(two, self.send_y)


def kernel(
    states, first, mods, coef, embed, qkv_pieces, out_pieces, final, adv_out, err_out,
    packed, messages, latents, edge, embed3, final2, qkv_rows, out_rows, modulated, accum,
    queries, key_rows, values, attended, gathered, updated, noise_own, noise_in, total, totals, part, parts,
    qkv_recv, qkv_send, qkv_send_y, out_recv, out_send, out_send_y,
    latent_recv, latent_send, edge_recv, edge_send, att_recv, att_send,
    noise_recv, noise_send, total_recv, total_send, part_recv, part_send,
):
    z = lax.axis_index("tm")
    s = lax.axis_index("seq")
    c = lax.rem(s, 2)
    x = lax.rem(s // 2, COLS)
    y = s // 8
    j = lax.rem(s, 8)
    parity = lax.rem(z, 2)
    place = (z, x, y, c, parity)
    above = lax.rem(z + 1, PLANES)
    below = lax.rem(z + PLANES - 1, PLANES)

    barrier = pltpu.get_barrier_semaphore()

    def greet(o, carry):
        pl.semaphore_signal(barrier, inc=1, device_id=(z, lax.rem(s + o, PEERS)), device_id_type=MESH)
        return carry

    lax.fori_loop(1, PEERS, greet, 0)

    def greet_column(o, carry):
        pl.semaphore_signal(barrier, inc=1, device_id=(lax.rem(z + o, PLANES), s), device_id_type=MESH)
        return carry

    lax.fori_loop(1, PLANES, greet_column, 0)
    pl.semaphore_signal(barrier, inc=1, device_id=(below, y * 8 + 7), device_id_type=MESH)

    start = pack(first[...])
    for t in range(STEPS):
        block = pack(states[t])
        packed[t] = block
        if t == STEPS - 1:
            block = jnp.where(z == PLANES - 1, start, block)
        messages[t] = block.astype(BF16)
    embed3[...] = jnp.zeros_like(embed3)
    for third in range(3):
        embed3[third, third * CH : (third + 1) * CH, :] = embed[...]
    weight = final[...]
    final2[0] = jnp.concatenate([weight, jnp.zeros((D, CH), BF16)], axis=1)
    final2[1] = jnp.concatenate([jnp.zeros((D, CH), BF16), weight], axis=1)
    for head in range(GROUP):
        values[head, :, HD:] = jnp.ones((D, HD), BF16)

    pl.semaphore_wait(barrier, jnp.where(j == 7, 46, 38))

    def latent_slot(k):
        return latents.at[pl.ds(pl.multiple_of(k * PACK, PACK), PACK)]

    def send_latent(o, carry):
        peer = lax.rem(s + o, PEERS)
        pltpu.make_async_remote_copy(
            messages.at[lax.rem(peer, 8)], latent_slot(s), latent_send, latent_recv,
            device_id=(z, peer), device_id_type=MESH,
        ).start()
        return carry

    lax.fori_loop(1, PEERS, send_latent, 0)
    pltpu.make_async_copy(messages.at[j], latent_slot(s), latent_recv).start()

    qkv = Spread(place, qkv_pieces, qkv_rows, qkv_recv, qkv_send, qkv_send_y, False)
    out = Spread(place, out_pieces, out_rows, out_recv, out_send, out_send_y, True)
    qkv.stage_y()
    edge_copy = pltpu.make_async_remote_copy(
        packed.at[STEPS - 1], edge, edge_send, edge_recv, device_id=(above, s), device_id_type=MESH
    )
    edge_copy.start()
    qkv.own(0)
    qkv.own(1)
    await_bytes(latents, latent_recv)

    def mod_row(kind, start, size):
        return mods[pl.ds(j, 1), pl.ds(pl.multiple_of(kind * D + start, 128), size)]

    def make_modulated(quarter):
        rows = latents[quarter * QROW : (quarter + 1) * QROW, :]

        def one(third, carry):
            chunks = []
            for k in range(4):
                at = lax.rem(y + qkv.up(k), ROWS) * QTOK
                chunks.append(
                    jnp.dot(
                        rows, embed3[third, :, pl.ds(pl.multiple_of(at, 128), QTOK)],
                        preferred_element_type=F32,
                    )
                )
            row_mean = sum(jnp.sum(v, axis=1, keepdims=True) for v in chunks) / D
            chunks = [v - row_mean for v in chunks]
            variance = sum(jnp.sum(v * v, axis=1, keepdims=True) for v in chunks) / D
            inverse = lax.rsqrt(variance + 1e-06)
            base = pl.multiple_of(quarter * QTOK + third * QROW, QROW)
            for k in range(4):
                at = lax.rem(y + qkv.up(k), ROWS) * QTOK
                modulated[pl.ds(base, QROW), k * QTOK : (k + 1) * QTOK] = (
                    chunks[k] * inverse * (1.0 + mod_row(1, at, QTOK)) + mod_row(0, at, QTOK)
                ).astype(BF16)
            return carry

        lax.fori_loop(0, 3, one, 0)

    make_modulated(0)
    qkv.from_left(0)
    qkv.from_right(0)
    make_modulated(1)
    qkv.from_left(1)
    qkv.from_right(1)
    make_modulated(2)
    qkv.far(0)
    make_modulated(3)
    qkv.far(1)
    out.stage_y()
    qkv.await_sibling(0)
    qkv.await_sibling(1)

    def project_first(i, carry):
        at = pl.ds(pl.multiple_of(i * 256, 256), 256)
        accum[at, :] = jnp.dot(modulated[at, : D // 2], qkv_rows[: D // 2, :], preferred_element_type=F32)
        return carry

    lax.fori_loop(0, 2, project_first, 0)
    for k in (2, 3):
        qkv.from_plane(k, 0)
    lax.fori_loop(2, 4, project_first, 0)
    for k in (2, 3):
        qkv.from_plane(k, -1)
        qkv.from_plane(k, 1)
    lax.fori_loop(4, 6, project_first, 0)
    for k in (2, 3):
        qkv.from_plane(k, 2)
    out.own(0)
    out.own(1)
    qkv.await_sibling(2)
    qkv.await_sibling(3)

    scale = HD ** (-0.5) * math.log2(math.e)

    def project_second(i, carry):
        at = pl.ds(pl.multiple_of(i * 256, 256), 256)
        whole = accum[at, :] + jnp.dot(
            modulated[at, D // 2 :], qkv_rows[D // 2 :, :], preferred_element_type=F32
        )
        for head in range(GROUP):
            base = head * 3 * HD
            queries[head, at, :] = (whole[:, base : base + HD] * scale).astype(BF16)
            key_rows[head, at, :] = whole[:, base + HD : base + 2 * HD].astype(BF16)
            values[head, at, :HD] = whole[:, base + 2 * HD : base + 3 * HD].astype(BF16)
        return carry

    lax.fori_loop(0, 3, project_second, 0)
    out.from_left(0)
    out.from_right(0)
    lax.fori_loop(3, 6, project_second, 0)
    out.from_left(1)
    out.from_right(1)

    def attend(head):
        column = pl.ds(pl.multiple_of((y * GROUP + head) * HD, HD), HD)

        def one(i, carry):
            quarter = lax.rem(y + 1 + i, ROWS)
            block = queries[head, pl.ds(pl.multiple_of(quarter * QTOK, QTOK), QTOK), :]
            scores = lax.dot_general(
                block, key_rows[head], (((1,), (1,)), ((), ())), preferred_element_type=F32
            )
            row_max = jnp.max(scores, axis=1, keepdims=True)
            weights = jnp.exp2(scores - row_max).astype(BF16)
            both = jnp.dot(weights, values[head], preferred_element_type=F32)
            attended[head * ROWS + i] = (both[:, :HD] / both[:, HD:]).astype(BF16)

            @pl.when(i < 3)
            def _():
                pltpu.make_async_remote_copy(
                    attended.at[head * ROWS + i], gathered.at[:, column], att_send, att_recv,
                    device_id=(z, quarter * 8 + j), device_id_type=MESH,
                ).start()

            @pl.when(i == 3)
            def _():
                pltpu.make_async_copy(attended.at[head * ROWS + i], gathered.at[:, column], att_recv).start()

            return carry

        lax.fori_loop(0, ROWS, one, 0)

    attend(0)
    out.far(0)
    out.far(1)
    for k in (2, 3):
        out.from_plane(k, 0)
    attend(1)
    for k in (2, 3):
        out.from_plane(k, -1)
        out.from_plane(k, 1)
        out.from_plane(k, 2)
    attend(2)
    for k in range(4):
        out.await_sibling(k)
    await_bytes(gathered, att_recv)

    for n in range(3):
        at = slice(n * 512, (n + 1) * 512)
        updated[:, at] = jnp.dot(gathered[...], out_rows[:, at], preferred_element_type=F32)

    normed = []
    own_rows = latents[pl.ds(pl.multiple_of(y * QROW, QROW), QROW), :]
    for third in range(3):
        residual = jnp.dot(own_rows, embed3[third], preferred_element_type=F32)
        moved = residual + mod_row(2, 0, D) * updated[third * QROW : (third + 1) * QROW, :]
        normed.append(layer_norm(moved).astype(BF16))
    near = jnp.dot(normed[0], final2[0], preferred_element_type=F32)
    near = near + jnp.dot(normed[1], final2[1], preferred_element_type=F32)
    rest = jnp.dot(normed[2], final2[0], preferred_element_type=F32)
    for k in range(8):
        at = slice(k * PACK, (k + 1) * PACK)
        noise_own[k, :, :HD] = near[at]
        noise_own[k, :, HD:] = rest[at]

    arrive = lax.rem(j + 1, STEPS)
    plane = jnp.where(j == 7, above, z)
    for k in range(8):
        mine = jnp.logical_and(j != 7, j == k)

        @pl.when(jnp.logical_not(mine))
        def _():
            pltpu.make_async_remote_copy(
                noise_own.at[k], noise_in.at[arrive], noise_send, noise_recv,
                device_id=(plane, y * 8 + k), device_id_type=MESH,
            ).start()

        @pl.when(mine)
        def _():
            pltpu.make_async_copy(noise_own.at[k], noise_in.at[arrive], noise_recv).start()

    edge_copy.wait_recv()
    before = jnp.where(z == 0, start, edge[...])
    await_bytes(noise_in, noise_recv)

    running = jnp.zeros((PACK, LANES), F32)
    sums = []
    for t in range(STEPS):
        previous = before if t == 0 else packed[t - 1]
        running = running + (coef[t : t + 1, :] * previous + coef[STEPS + t : STEPS + t + 1, :] * noise_in[t])
        sums.append(running)
    total[...] = running
    for o in range(1, PLANES):

        @pl.when(z + o < PLANES)
        def _():
            pltpu.make_async_remote_copy(
                total, totals.at[z], total_send.at[o], total_recv.at[z],
                device_id=(z + o, s), device_id_type=MESH,
            ).start()

    totals_sum = start
    for o in range(PLANES - 1):

        @pl.when(o < z)
        def _():
            await_bytes(totals.at[o], total_recv.at[o])

        @pl.when(o >= z)
        def _():
            totals[o] = jnp.zeros((PACK, LANES), F32)

        totals_sum = totals_sum + totals[o]

    squares = []
    for t in range(STEPS):
        advanced = totals_sum + sums[t]
        adv_out[t, 0:PACK, :] = advanced[:, 0:CH]
        adv_out[t, PACK : 2 * PACK, :] = advanced[:, CH : 2 * CH]
        adv_out[t, 2 * PACK :, :] = advanced[:, 2 * CH : 3 * CH]
        difference = advanced - packed[t]
        square = jnp.sum(difference * difference, axis=0, keepdims=True)
        squares.append(square[:, :HD] + square[:, HD:])
    part[...] = jnp.concatenate(squares, axis=0)

    def send_part(o, carry):
        pltpu.make_async_remote_copy(
            part, parts.at[s], part_send, part_recv,
            device_id=(z, lax.rem(s + o, PEERS)), device_id_type=MESH,
        ).start()
        return carry

    lax.fori_loop(1, PEERS, send_part, 0)
    pltpu.make_async_copy(part, parts.at[s], part_recv).start()
    await_bytes(parts, part_recv)
    summed = jnp.sum(jnp.sum(parts[...], axis=0), axis=1, keepdims=True) / (D * CH)
    err_out[...] = jnp.broadcast_to(summed, (STEPS, HD))

    qkv.finish()
    out.finish()
    await_bytes(latents.at[pl.ds(0, (PEERS - 1) * PACK)], latent_send)
    edge_copy.wait_send()
    await_bytes(attended.at[pl.ds(0, 9)], att_send)

    @pl.when(j == 7)
    def _():
        await_bytes(noise_in, noise_send)

    @pl.when(j != 7)
    def _():
        await_bytes(noise_in.at[pl.ds(0, 7)], noise_send)

    for o in range(1, PLANES):

        @pl.when(z + o < PLANES)
        def _():
            await_bytes(total, total_send.at[o])

    await_bytes(parts.at[pl.ds(0, PEERS - 1)], part_send)


def per_device(
    states, first_state, now_step, next_step, embed_weight, mod_weight, qkv_weight, out_weight, final_weight
):
    plane = lax.axis_index("tm")
    keep_coef, noise_coef = coefficients(now_step, next_step)
    coef = jnp.broadcast_to(jnp.concatenate([keep_coef, noise_coef])[:, None], (2 * STEPS, LANES))
    last = jnp.logical_and(plane == PLANES - 1, jnp.arange(STEPS) == STEPS - 1)
    mods = modulation(jnp.where(last, 960, next_step), mod_weight)
    qkv_pieces = jnp.transpose(qkv_weight.reshape(TOK, ROWS, GROUP * 3 * HD), (1, 0, 2))
    out_pieces = out_weight[None]
    dma = pltpu.SemaphoreType.DMA
    vmem = pltpu.VMEM
    advanced, errors = pl.pallas_call(
        kernel,
        out_shape=(
            jax.ShapeDtypeStruct((STEPS, TOK, CH), F32),
            jax.ShapeDtypeStruct((STEPS, HD), F32),
        ),
        in_specs=[pl.BlockSpec(memory_space=pltpu.VMEM)] * 8,
        out_specs=(pl.BlockSpec(memory_space=pltpu.VMEM),) * 2,
        scratch_shapes=[
            vmem((STEPS, PACK, LANES), F32),
            vmem((STEPS, PACK, LANES), BF16),
            vmem((PEERS * PACK, LANES), BF16),
            vmem((PACK, LANES), F32),
            vmem((3, LANES, D), BF16),
            vmem((2, D, HD), BF16),
            vmem((D, GROUP * 3 * HD), BF16),
            vmem((D, D), BF16),
            vmem((D, D), BF16),
            vmem((D, GROUP * 3 * HD), F32),
            vmem((GROUP, D, HD), BF16),
            vmem((GROUP, D, HD), BF16),
            vmem((GROUP, D, 2 * HD), BF16),
            vmem((GROUP * ROWS, QTOK, HD), BF16),
            vmem((QTOK, D), BF16),
            vmem((QTOK, D), F32),
            vmem((8, PACK, LANES), F32),
            vmem((STEPS, PACK, LANES), F32),
            vmem((PACK, LANES), F32),
            vmem((PLANES, PACK, LANES), F32),
            vmem((STEPS, HD), F32),
            vmem((PEERS, STEPS, HD), F32),
            dma((PEERS,)), dma, dma,
            dma((PEERS,)), dma, dma,
            dma, dma, dma, dma, dma, dma,
            dma, dma, dma((PLANES,)), dma((PLANES,)), dma, dma,
        ],
        compiler_params=pltpu.CompilerParams(
            collective_id=0, has_side_effects=True, vmem_limit_bytes=60 * 1024 * 1024
        ),
        name="picard",
    )(states, first_state, mods, coef, embed_weight, qkv_pieces, out_pieces, final_weight)
    return advanced, errors[:, 0]


def solution(mesh):
    in_specs = (
        P("tm", "seq", None),
        P("seq", None),
        P("tm"),
        P("tm"),
        P(),
        P(),
        P("seq", None, None),
        P("seq", None),
        P(),
    )
    out_specs = (P("tm", "seq", None), P("tm"))
    return jax.shard_map(
        per_device, mesh=mesh, in_specs=in_specs, out_specs=out_specs, check_vma=False
    )
```

```python
import math

import jax
import jax.numpy as jnp
from jax import lax
from jax.experimental import pallas as pl
from jax.experimental.pallas import tpu as pltpu
from jax.sharding import PartitionSpec as P

MESH = pl.DeviceIdType.MESH
F32 = jnp.float32
BF16 = jnp.bfloat16

PLANES = 8
ROWS = 4
COLS = 4
PEERS = 32
STEPS = 8
TOK = 48
PACK = 16
CH = 64
D = 1536
HD = 128
HEADS = 12
GROUP = 3
QTOK = 384
QROW = 128
LANES = 256


def alpha_bar(step_ids):
    fraction = (step_ids.astype(F32) / 1000.0 + 0.008) / 1.008
    return jnp.cos(fraction * (math.pi / 2)) ** 2


def coefficients(now_step, next_step):
    alpha_now = alpha_bar(now_step)
    alpha_next = alpha_bar(next_step)
    step_ratio = jnp.sqrt(alpha_next / alpha_now)
    keep_coef = step_ratio - 1.0
    noise_coef = jnp.sqrt(1.0 - alpha_next) - step_ratio * jnp.sqrt(1.0 - alpha_now)
    return (keep_coef, noise_coef)


def on_rows(steps):
    row = lax.broadcasted_iota(jnp.int32, (STEPS, HD), 0)
    spread = jnp.zeros((STEPS, HD), jnp.int32)
    for t in range(STEPS):
        spread = jnp.where(row == t, steps[t], spread)
    return spread


def await_bytes(ref, sem):
    pltpu.make_async_copy(ref, ref, sem).wait()


def layer_norm(rows):
    row_mean = jnp.mean(rows, axis=-1, keepdims=True)
    centered = rows - row_mean
    variance = jnp.mean(centered * centered, axis=-1, keepdims=True)
    return centered * lax.rsqrt(variance + 1e-06)


def pack(tokens):
    first = jnp.concatenate([tokens[0:PACK], tokens[PACK : 2 * PACK]], axis=1)
    second = jnp.concatenate([tokens[2 * PACK :], jnp.zeros((PACK, CH), F32)], axis=1)
    return jnp.concatenate([first, second], axis=1)


class Spread:
    def __init__(self, place, pieces, whole, recv, send, send_y, natural):
        self.z, self.x, self.y, self.c, self.parity = place
        self.pieces, self.whole, self.natural = pieces, whole, natural
        self.recv, self.send, self.send_y = recv, send, send_y

    def up(self, k):
        return self.parity + 2 * k if k < 2 else (1 - self.parity) + 2 * (k - 2)

    def slot(self, k, xx, cc):
        major = lax.rem(self.y + self.up(k), ROWS) if self.natural else k
        return major * 8 + xx * 2 + cc

    def rows(self, slot):
        return self.whole.at[pl.ds(pl.multiple_of(slot * TOK, 16), TOK)]

    def await_slot(self, slot):
        await_bytes(self.rows(slot), self.recv.at[slot])

    def stage_y(self):
        for k in range(2):
            up = self.up(k)
            target = lax.rem(self.y - up + ROWS, ROWS)
            here = self.slot(k, self.x, self.c)
            there = (self.y if self.natural else k) * 8 + self.x * 2 + self.c
            source = self.pieces.at[target] if self.pieces.shape[0] > 1 else self.pieces.at[0]

            def remote():
                pltpu.make_async_remote_copy(
                    source, self.rows(there), self.send_y, self.recv.at[there],
                    device_id=(self.z, target * 8 + self.x * 2 + self.c), device_id_type=MESH,
                ).start()

            if k == 0:
                pl.when(self.parity == 1)(remote)

                @pl.when(self.parity == 0)
                def _():
                    pltpu.make_async_copy(source, self.rows(here), self.recv.at[here]).start()
            else:
                remote()

    def pass_on(self, slot, there, plane, xx, cc):
        pltpu.make_async_remote_copy(
            self.rows(slot), self.rows(there), self.send, self.recv.at[there],
            device_id=(plane, self.y * 8 + xx * 2 + cc), device_id_type=MESH,
        ).start()

    def side(self, by):
        return lax.rem(self.x + by + COLS, COLS)

    def to_plane(self, k, xx):
        plane = lax.rem(self.z + (1 if k == 0 else PLANES - 1), PLANES)
        slot = self.slot(k, xx, self.c)
        there = slot if self.natural else slot + 16
        self.pass_on(slot, there, plane, self.x, self.c)

    def to_sibling(self, slot):
        self.pass_on(slot, slot, self.z, self.x, 1 - self.c)

    def own(self, k):
        slot = self.slot(k, self.x, self.c)
        self.await_slot(slot)
        self.pass_on(slot, slot, self.z, self.side(1), self.c)
        self.pass_on(slot, slot, self.z, self.side(-1), self.c)
        self.to_plane(k, self.x)
        self.to_sibling(slot)

    def from_left(self, k):
        slot = self.slot(k, self.side(-1), self.c)
        self.await_slot(slot)
        if k == 0:
            self.pass_on(slot, slot, self.z, self.side(1), self.c)
        self.to_plane(k, self.side(-1))
        self.to_sibling(slot)

    def from_right(self, k):
        slot = self.slot(k, self.side(1), self.c)
        self.await_slot(slot)
        if k == 1:
            self.pass_on(slot, slot, self.z, self.side(-1), self.c)
        self.to_plane(k, self.side(1))
        self.to_sibling(slot)

    def far(self, k):
        slot = self.slot(k, self.side(2), self.c)
        self.await_slot(slot)
        self.to_plane(k, self.side(2))
        self.to_sibling(slot)

    def from_plane(self, k, by):
        slot = self.slot(k, self.side(by), self.c)
        self.await_slot(slot)
        self.to_sibling(slot)

    def await_sibling(self, k):
        for xx in range(COLS):
            self.await_slot(self.slot(k, xx, 1 - self.c))

    def finish(self):
        await_bytes(self.whole.at[pl.ds(0, 30 * TOK)], self.send)
        one = self.whole.at[pl.ds(0, TOK)]
        two = self.whole.at[pl.ds(0, 2 * TOK)]

        @pl.when(self.parity == 0)
        def _():
            await_bytes(one, self.send_y)

        @pl.when(self.parity == 1)
        def _():
            await_bytes(two, self.send_y)


def kernel(
    states, first, now_step, next_step, embed, mod_weight, qkv_heads, out_pieces, final, adv_out, err_out,
    mod_rows, mods, coef, qkv_pieces, packed, messages, latents, edge, embed3, final2, qkv_rows, out_rows, modulated, accum,
    queries, key_rows, values, attended, gathered, updated, noise_own, noise_in, total, totals, part, parts,
    qkv_recv, qkv_send, qkv_send_y, out_recv, out_send, out_send_y,
    latent_recv, latent_send, edge_recv, edge_send, att_recv, att_send,
    noise_recv, noise_send, mod_sem, total_recv, total_send, part_recv, part_send,
):
    z = lax.axis_index("tm")
    s = lax.axis_index("seq")
    c = lax.rem(s, 2)
    x = lax.rem(s // 2, COLS)
    y = s // 8
    j = lax.rem(s, 8)
    parity = lax.rem(z, 2)
    place = (z, x, y, c, parity)
    above = lax.rem(z + 1, PLANES)
    below = lax.rem(z + PLANES - 1, PLANES)

    barrier = pltpu.get_barrier_semaphore()

    def greet(o, carry):
        pl.semaphore_signal(barrier, inc=1, device_id=(z, lax.rem(s + o, PEERS)), device_id_type=MESH)
        return carry

    lax.fori_loop(1, PEERS, greet, 0)

    def greet_column(o, carry):
        pl.semaphore_signal(barrier, inc=1, device_id=(lax.rem(z + o, PLANES), s), device_id_type=MESH)
        return carry

    lax.fori_loop(1, PLANES, greet_column, 0)
    pl.semaphore_signal(barrier, inc=1, device_id=(below, y * 8 + 7), device_id_type=MESH)

    mod_copy = pltpu.make_async_copy(mod_weight, mod_rows, mod_sem)
    mod_copy.start()
    start = pack(first[...])
    for t in range(STEPS):
        block = pack(states[t])
        packed[t] = block
        if t == STEPS - 1:
            block = jnp.where(z == PLANES - 1, start, block)
        messages[t] = block.astype(BF16)
    embed3[...] = jnp.zeros_like(embed3)
    for third in range(3):
        embed3[third, third * CH : (third + 1) * CH, :] = embed[...]
    final2[...] = jnp.zeros_like(final2)
    final2[0, :CH, :] = final[...]
    final2[1, CH:, :] = final[...]
    for group in range(ROWS):
        for head in range(GROUP):
            qkv_pieces[group, :, head * 3 * HD : (head + 1) * 3 * HD] = qkv_heads[group * GROUP + head]
    for head in range(GROUP):
        values[head, :, HD:] = jnp.ones((D, HD), BF16)

    keep_coef, noise_coef = coefficients(on_rows(now_step), on_rows(next_step))
    for half in range(2):
        coef[:STEPS, half * HD : (half + 1) * HD] = keep_coef
        coef[STEPS:, half * HD : (half + 1) * HD] = noise_coef
    step = jnp.where(jnp.logical_and(z == PLANES - 1, j == STEPS - 1), 960, next_step[j])
    lane = lax.broadcasted_iota(jnp.int32, (STEPS, HD), 1).astype(F32)
    angles = step.astype(F32) * jnp.exp(-math.log(10000.0) * lane / HD)
    time_embed = jnp.concatenate([jnp.cos(angles), jnp.sin(angles)], axis=1).astype(BF16)
    mod_copy.wait()
    for n in range(3):
        at = slice(n * D, (n + 1) * D)
        mods[:, at] = jnp.dot(time_embed, mod_rows[:, at], preferred_element_type=F32)

    pl.semaphore_wait(barrier, jnp.where(j == 7, 46, 38))

    def latent_slot(k):
        return latents.at[pl.ds(pl.multiple_of(k * PACK, PACK), PACK)]

    def send_latent(o, carry):
        peer = lax.rem(s + o, PEERS)
        pltpu.make_async_remote_copy(
            messages.at[lax.rem(peer, 8)], latent_slot(s), latent_send, latent_recv,
            device_id=(z, peer), device_id_type=MESH,
        ).start()
        return carry

    lax.fori_loop(1, PEERS, send_latent, 0)
    pltpu.make_async_copy(messages.at[j], latent_slot(s), latent_recv).start()

    qkv = Spread(place, qkv_pieces, qkv_rows, qkv_recv, qkv_send, qkv_send_y, False)
    out = Spread(place, out_pieces, out_rows, out_recv, out_send, out_send_y, True)
    qkv.stage_y()
    edge_copy = pltpu.make_async_remote_copy(
        packed.at[STEPS - 1], edge, edge_send, edge_recv, device_id=(above, s), device_id_type=MESH
    )
    edge_copy.start()
    qkv.own(0)
    qkv.own(1)
    qkv.from_left(0)
    qkv.from_right(0)
    await_bytes(latents, latent_recv)

    def mod_row(kind, start, size):
        return mods[0:1, pl.ds(pl.multiple_of(kind * D + start, 128), size)]

    def make_modulated(quarter):
        rows = latents[quarter * QROW : (quarter + 1) * QROW, :]

        def one(third, carry):
            chunks = []
            for k in range(4):
                at = lax.rem(y + qkv.up(k), ROWS) * QTOK
                chunks.append(
                    jnp.dot(
                        rows, embed3[third, :, pl.ds(pl.multiple_of(at, 128), QTOK)],
                        preferred_element_type=F32,
                    )
                )
            row_mean = sum(jnp.sum(v, axis=1, keepdims=True) for v in chunks) / D
            chunks = [v - row_mean for v in chunks]
            variance = sum(jnp.sum(v * v, axis=1, keepdims=True) for v in chunks) / D
            inverse = lax.rsqrt(variance + 1e-06)
            base = pl.multiple_of(quarter * QTOK + third * QROW, QROW)
            for k in range(4):
                at = lax.rem(y + qkv.up(k), ROWS) * QTOK
                modulated[pl.ds(base, QROW), k * QTOK : (k + 1) * QTOK] = (
                    chunks[k] * inverse * (1.0 + mod_row(1, at, QTOK)) + mod_row(0, at, QTOK)
                ).astype(BF16)
            return carry

        lax.fori_loop(0, 3, one, 0)

    make_modulated(0)
    qkv.from_left(1)
    qkv.from_right(1)
    make_modulated(1)
    qkv.far(0)
    make_modulated(2)
    qkv.far(1)
    out.stage_y()
    make_modulated(3)
    qkv.from_plane(2, 0)
    qkv.from_plane(3, 0)
    qkv.await_sibling(0)
    qkv.await_sibling(1)

    def project_first(i, carry):
        at = pl.ds(pl.multiple_of(i * 256, 256), 256)
        accum[at, :] = jnp.dot(modulated[at, : D // 2], qkv_rows[: D // 2, :], preferred_element_type=F32)
        return carry

    lax.fori_loop(0, 2, project_first, 0)
    qkv.from_plane(2, -1)
    qkv.from_plane(2, 1)
    lax.fori_loop(2, 4, project_first, 0)
    qkv.from_plane(3, -1)
    qkv.from_plane(3, 1)
    lax.fori_loop(4, 6, project_first, 0)
    qkv.from_plane(2, 2)
    qkv.from_plane(3, 2)
    out.own(0)
    out.own(1)
    qkv.await_sibling(2)
    qkv.await_sibling(3)

    scale = HD ** (-0.5) * math.log2(math.e)

    def project_second(i, carry):
        at = pl.ds(pl.multiple_of(i * 256, 256), 256)
        whole = accum[at, :] + jnp.dot(
            modulated[at, D // 2 :], qkv_rows[D // 2 :, :], preferred_element_type=F32
        )
        for head in range(GROUP):
            base = head * 3 * HD
            queries[head, at, :] = (whole[:, base : base + HD] * scale).astype(BF16)
            key_rows[head, at, :] = whole[:, base + HD : base + 2 * HD].astype(BF16)
            values[head, at, :HD] = whole[:, base + 2 * HD : base + 3 * HD].astype(BF16)
        return carry

    lax.fori_loop(0, 3, project_second, 0)
    out.from_left(0)
    out.from_right(0)
    lax.fori_loop(3, 6, project_second, 0)
    out.from_left(1)
    out.from_right(1)

    def attend(i):
        quarter = lax.rem(y + 1 + i, ROWS)

        def one(head, carry):
            column = pl.ds(pl.multiple_of((y * GROUP + head) * HD, HD), HD)
            block = queries[head, pl.ds(pl.multiple_of(quarter * QTOK, QTOK), QTOK), :]
            scores = lax.dot_general(
                block, key_rows[head], (((1,), (1,)), ((), ())), preferred_element_type=F32
            )
            row_max = jnp.max(scores, axis=1, keepdims=True)
            weights = jnp.exp2(scores - row_max).astype(BF16)
            both = jnp.dot(weights, values[head], preferred_element_type=F32)
            attended[i * GROUP + head] = (both[:, :HD] / both[:, HD:]).astype(BF16)
            source = attended.at[i * GROUP + head]
            if i < 3:
                pltpu.make_async_remote_copy(
                    source, gathered.at[:, column], att_send, att_recv,
                    device_id=(z, quarter * 8 + j), device_id_type=MESH,
                ).start()
            else:
                pltpu.make_async_copy(source, gathered.at[:, column], att_recv).start()
            return carry

        lax.fori_loop(0, GROUP, one, 0)

    attend(0)
    out.far(0)
    out.far(1)
    out.from_plane(2, 0)
    out.from_plane(3, 0)
    attend(1)
    out.from_plane(2, -1)
    out.from_plane(2, 1)
    out.from_plane(3, -1)
    out.from_plane(3, 1)
    attend(2)
    out.from_plane(2, 2)
    out.from_plane(3, 2)
    attend(3)
    for k in range(4):
        out.await_sibling(k)
    await_bytes(gathered, att_recv)

    for n in range(3):
        at = slice(n * 512, (n + 1) * 512)
        updated[:, at] = jnp.dot(gathered[...], out_rows[:, at], preferred_element_type=F32)

    normed = []
    own_rows = latents[pl.ds(pl.multiple_of(y * QROW, QROW), QROW), :]
    for third in range(3):
        residual = jnp.dot(own_rows, embed3[third], preferred_element_type=F32)
        moved = residual + mod_row(2, 0, D) * updated[third * QROW : (third + 1) * QROW, :]
        normed.append(layer_norm(moved).astype(BF16))

    def to_noise(rows, half):
        return lax.dot_general(rows, final2[half], (((1,), (1,)), ((), ())), preferred_element_type=F32)

    near = (to_noise(normed[0], 0) + to_noise(normed[1], 1)).astype(BF16)
    rest = to_noise(normed[2], 0).astype(BF16)
    for k in range(8):
        at = slice(k * PACK, (k + 1) * PACK)
        noise_own[k, :, :HD] = near[at]
        noise_own[k, :, HD:] = rest[at]

    arrive = lax.rem(j + 1, STEPS)
    plane = jnp.where(j == 7, above, z)
    for k in range(8):
        mine = jnp.logical_and(j != 7, j == k)

        @pl.when(jnp.logical_not(mine))
        def _():
            pltpu.make_async_remote_copy(
                noise_own.at[k], noise_in.at[arrive], noise_send, noise_recv,
                device_id=(plane, y * 8 + k), device_id_type=MESH,
            ).start()

        @pl.when(mine)
        def _():
            pltpu.make_async_copy(noise_own.at[k], noise_in.at[arrive], noise_recv).start()

    edge_copy.wait_recv()
    before = jnp.where(z == 0, start, edge[...])
    await_bytes(noise_in, noise_recv)

    running = jnp.zeros((PACK, LANES), F32)
    sums = []
    for t in range(STEPS):
        previous = before if t == 0 else packed[t - 1]
        running = running + (coef[t : t + 1, :] * previous + coef[STEPS + t : STEPS + t + 1, :] * noise_in[t].astype(F32))
        sums.append(running)
    total[...] = running
    for o in range(1, PLANES):

        @pl.when(z + o < PLANES)
        def _():
            pltpu.make_async_remote_copy(
                total, totals.at[z], total_send.at[o], total_recv.at[z],
                device_id=(z + o, s), device_id_type=MESH,
            ).start()

    totals_sum = start
    for o in range(PLANES - 1):

        @pl.when(o < z)
        def _():
            await_bytes(totals.at[o], total_recv.at[o])

        @pl.when(o >= z)
        def _():
            totals[o] = jnp.zeros((PACK, LANES), F32)

        totals_sum = totals_sum + totals[o]

    squares = []
    for t in range(STEPS):
        advanced = totals_sum + sums[t]
        adv_out[t, 0:PACK, :] = advanced[:, 0:CH]
        adv_out[t, PACK : 2 * PACK, :] = advanced[:, CH : 2 * CH]
        adv_out[t, 2 * PACK :, :] = advanced[:, 2 * CH : 3 * CH]
        difference = advanced - packed[t]
        square = jnp.sum(difference * difference, axis=0, keepdims=True)
        squares.append(square[:, :HD] + square[:, HD:])
    part[...] = jnp.concatenate(squares, axis=0)

    def send_part(o, carry):
        pltpu.make_async_remote_copy(
            part, parts.at[s], part_send, part_recv,
            device_id=(z, lax.rem(s + o, PEERS)), device_id_type=MESH,
        ).start()
        return carry

    lax.fori_loop(1, PEERS, send_part, 0)
    pltpu.make_async_copy(part, parts.at[s], part_recv).start()
    await_bytes(parts, part_recv)
    summed = jnp.sum(jnp.sum(parts[...], axis=0), axis=1, keepdims=True) / (D * CH)
    row = lax.broadcasted_iota(jnp.int32, (STEPS, HD), 0)
    lane = lax.broadcasted_iota(jnp.int32, (STEPS, HD), 1)
    err_out[...] = jnp.sum(jnp.where(row == lane, summed, 0.0), axis=0, keepdims=True)

    qkv.finish()
    out.finish()
    await_bytes(latents.at[pl.ds(0, (PEERS - 1) * PACK)], latent_send)
    edge_copy.wait_send()
    await_bytes(attended.at[pl.ds(0, 9)], att_send)

    @pl.when(j == 7)
    def _():
        await_bytes(noise_in, noise_send)

    @pl.when(j != 7)
    def _():
        await_bytes(noise_in.at[pl.ds(0, 7)], noise_send)

    for o in range(1, PLANES):

        @pl.when(z + o < PLANES)
        def _():
            await_bytes(total, total_send.at[o])

    await_bytes(parts.at[pl.ds(0, PEERS - 1)], part_send)


def per_device(
    states, first_state, now_step, next_step, embed_weight, mod_weight, qkv_weight, out_weight, final_weight
):
    vmem_in = pl.BlockSpec(memory_space=pltpu.VMEM)
    smem_in = pl.BlockSpec(memory_space=pltpu.SMEM)
    hbm_in = pl.BlockSpec(memory_space=pltpu.HBM)
    dma = pltpu.SemaphoreType.DMA
    vmem = pltpu.VMEM
    advanced, errors = pl.pallas_call(
        kernel,
        out_shape=(
            jax.ShapeDtypeStruct((STEPS, TOK, CH), F32),
            jax.ShapeDtypeStruct((1, HD), F32),
        ),
        in_specs=[vmem_in, vmem_in, smem_in, smem_in, vmem_in, hbm_in, vmem_in, vmem_in, vmem_in],
        out_specs=(pl.BlockSpec(memory_space=pltpu.VMEM),) * 2,
        scratch_shapes=[
            vmem((256, 3 * D), BF16),
            vmem((STEPS, 3 * D), F32),
            vmem((2 * STEPS, LANES), F32),
            vmem((ROWS, TOK, GROUP * 3 * HD), BF16),
            vmem((STEPS, PACK, LANES), F32),
            vmem((STEPS, PACK, LANES), BF16),
            vmem((PEERS * PACK, LANES), BF16),
            vmem((PACK, LANES), F32),
            vmem((3, LANES, D), BF16),
            vmem((2, HD, D), BF16),
            vmem((D, GROUP * 3 * HD), BF16),
            vmem((D, D), BF16),
            vmem((D, D), BF16),
            vmem((D, GROUP * 3 * HD), F32),
            vmem((GROUP, D, HD), BF16),
            vmem((GROUP, D, HD), BF16),
            vmem((GROUP, D, 2 * HD), BF16),
            vmem((GROUP * ROWS, QTOK, HD), BF16),
            vmem((QTOK, D), BF16),
            vmem((QTOK, D), F32),
            vmem((8, PACK, LANES), BF16),
            vmem((STEPS, PACK, LANES), BF16),
            vmem((PACK, LANES), F32),
            vmem((PLANES, PACK, LANES), F32),
            vmem((STEPS, HD), F32),
            vmem((PEERS, STEPS, HD), F32),
            dma((PEERS,)), dma, dma,
            dma((PEERS,)), dma, dma,
            dma, dma, dma, dma, dma, dma,
            dma, dma, dma, dma((PLANES,)), dma((PLANES,)), dma, dma,
        ],
        compiler_params=pltpu.CompilerParams(
            collective_id=0, has_side_effects=True, vmem_limit_bytes=60 * 1024 * 1024
        ),
        name="picard",
    )(
        states, first_state, now_step, next_step, embed_weight, mod_weight,
        jnp.transpose(qkv_weight, (1, 0, 2)), out_weight[None], final_weight.T,
    )
    return advanced, errors[0, :STEPS]


def solution(mesh):
    in_specs = (
        P("tm", "seq", None),
        P("seq", None),
        P("tm"),
        P("tm"),
        P(),
        P(),
        P("seq", None, None),
        P("seq", None),
        P(),
    )
    out_specs = (P("tm", "seq", None), P("tm"))
    return jax.shard_map(
        per_device, mesh=mesh, in_specs=in_specs, out_specs=out_specs, check_vma=False
    )
```
